32 devices in a mesh: cand: 4 (over y, core), hid: 8 (over z, x).
Axes of the slice: x: 2, y: 2, z: 4, core: 2. Of those that a mesh axis runs over, the one named last changes fastest.
Arguments:
- tokens: bfloat16 [4, 256, 2048], P('cand', None, 'hid'), may hold values from -6 to 6
- cotangent: bfloat16 [4, 256, 2048], P('cand', None, 'hid'), may hold values from -6 to 6
- gate_weight: bfloat16 [2048, 8192], P('cand', 'hid'), may hold values from -0.125 to 0.125
- up_weight: bfloat16 [2048, 8192], P('cand', 'hid'), may hold values from -0.125 to 0.125
- down_weight: bfloat16 [8192, 2048], P('hid', 'cand'), may hold values from -0.125 to 0.125
- width_steps: int32 [4], P('cand'), may hold values from 1 to 8
- block_order: int32 [8], replicated, may hold values from 0 to 7, each once
Outputs:
- grad_tokens: float32 [4, 256, 2048], P('cand', None, 'hid')
- grad_gate: float32 [2048, 8192], P('cand', 'hid')
- grad_up: float32 [2048, 8192], P('cand', 'hid')
- grad_down: float32 [8192, 2048], P('hid', 'cand')
The draws below stay inside these ranges and needn't reach their ends.
Inputs may be any that keep to these rules, and one draw needn't show every extreme that they name: Candidate c uses the first width_steps[c] * 1024 logical hidden units. `block_order`: names each of the 8 logical blocks once.
All inputs are finite; a program needn't handle non-finite values.
Results may differ from the reference program's by a relative error of at most 0.02.
Values may be sent and summed in bfloat16 or wider, within the bound.
A program may use at most 64 MiB of HBM per device.

```python
import jax
import jax.numpy as jnp
from jax import lax

D = 2048
FF = 8192
TOK = 256
CAND = 4
NBLK = 8
N_HID = 8


def place_ends(entries, key, smallest, high):
    place = [jax.random.randint(jax.random.fold_in(key, axis), (), 0, length) for axis, length in enumerate(entries.shape)]
    widest = entries.shape.index(max(entries.shape))
    neighbour = place[:widest] + [(place[widest] + 1) % entries.shape[widest]] + place[widest + 1:]
    return entries.at[tuple(place)].set(smallest).at[tuple(neighbour)].set(high)


def raised(drawn, stream_key, source, target, blocks, factor):
    owner, partner = [(jnp.arange(drawn.shape[position]) // (drawn.shape[position] // blocks)).reshape([-1 if axis == position else 1 for axis in range(drawn.ndim)]) for position in (source, target)]
    chosen = jax.random.permutation(stream_key, blocks)[partner]
    strong = (owner == chosen) | (owner == (partner + blocks // 2) % blocks)
    return jnp.where(strong, factor * drawn, drawn)


def steps_of(stream_key, shape, pieces, least, largest):
    def one(dim, blocks):
        heights = jax.random.uniform(jax.random.fold_in(jax.random.fold_in(stream_key, 6), dim), (blocks,), jnp.float32, least / len(pieces), largest / len(pieces))
        return jnp.repeat(jnp.exp(heights), shape[dim] // blocks).reshape((-1,) + (1,) * (len(shape) - dim - 1))

    loudness = one(*pieces[0])
    for cut in pieces[1:]:
        loudness = loudness * one(*cut)
    return loudness


def centred(key, dims, spread, most, shards=(), held_as=jnp.bfloat16):
    values = jax.random.normal(key, dims, jnp.float32) * spread
    if len(shards) > 0:
        values = steps_of(key, dims, shards, -0.22, 0.18) * values
    return jnp.clip(values, min=-most, max=most).astype(held_as)


def noise_with(key, dims, deviation, bound, shards, heavy, kind=jnp.bfloat16):
    entries = deviation * jax.random.normal(key, dims, jnp.float32)
    if shards:
        entries = entries * steps_of(key, dims, shards, -0.22, 0.18)
    return jnp.clip(raised(entries, jax.random.fold_in(key, 3), *heavy), -bound, bound).astype(kind)


def setup_inputs(seed: int = 0) -> dict:
    arg_keys = jax.random.split(jax.random.key(seed), 8)
    tokens = centred(arg_keys[0], (CAND, TOK, D), 1.0, 6.0, ((0, 4), (2, 8)))
    cotangent = noise_with(arg_keys[1], (CAND, TOK, D), 1.0, 6.0, ((0, 4), (2, 8)), (0, 2, 4, 2.0))
    gate_weight = centred(arg_keys[2], (D, FF), D ** -0.5, 0.125, ((0, 4), (1, 8)))
    up_weight = centred(arg_keys[3], (D, FF), D ** -0.5, 0.125, ((0, 4), (1, 8)))
    down_weight = centred(arg_keys[4], (FF, D), (FF // 4) ** -0.5, 0.125, ((0, 8), (1, 4)))
    width_steps = place_ends(jax.random.randint(arg_keys[5], (CAND,), 1, 9), jax.random.fold_in(arg_keys[5], 1), 1, 8).astype(jnp.int32)
    block_order = jax.random.permutation(arg_keys[6], NBLK).astype(jnp.int32)
    return {"tokens": tokens, "cotangent": cotangent, "gate_weight": gate_weight, "up_weight": up_weight, "down_weight": down_weight, "width_steps": width_steps, "block_order": block_order}


def reference(tokens, cotangent, gate_weight, up_weight, down_weight, width_steps, block_order):
    blk = FF // N_HID
    column = jnp.arange(FF, dtype=jnp.int32)
    logical = block_order[column // blk].astype(jnp.int32) * blk + column % blk
    gate_wide = gate_weight.astype(jnp.float32).reshape(D, N_HID, blk)
    up_wide = up_weight.astype(jnp.float32).reshape(D, N_HID, blk)

    def one(carry, index):
        inputs = tokens[index]
        upstream = cotangent[index]
        keep = (logical < width_steps[index] * (FF // 8)).astype(jnp.float32)
        gate = jnp.dot(inputs, gate_weight, preferred_element_type=jnp.float32)
        up = jnp.dot(inputs, up_weight, preferred_element_type=jnp.float32)
        sig = jax.nn.sigmoid(gate)
        act = keep * gate * sig
        hidden = (act * up).astype(jnp.bfloat16)
        dhid = keep * jnp.dot(upstream, down_weight.T, preferred_element_type=jnp.float32)
        d_up = (dhid * act).astype(jnp.bfloat16)
        d_gate = (dhid * up * keep * sig * (1.0 + gate * (1.0 - sig))).astype(jnp.bfloat16)
        down_c = jnp.dot(hidden.T, upstream, preferred_element_type=jnp.float32).astype(jnp.bfloat16).astype(jnp.float32)
        gate_c = jnp.dot(inputs.T, d_gate, preferred_element_type=jnp.float32).astype(jnp.bfloat16).astype(jnp.float32)
        up_c = jnp.dot(inputs.T, d_up, preferred_element_type=jnp.float32).astype(jnp.bfloat16).astype(jnp.float32)
        dg3 = d_gate.astype(jnp.float32).reshape(TOK, N_HID, blk)
        du3 = d_up.astype(jnp.float32).reshape(TOK, N_HID, blk)
        parts = jnp.einsum('tkb,dkb->ktd', dg3, gate_wide) + jnp.einsum('tkb,dkb->ktd', du3, up_wide)
        grad_in = jnp.sum(parts.astype(jnp.bfloat16).astype(jnp.float32), axis=0)
        return (carry[0] + gate_c, carry[1] + up_c, carry[2] + down_c), grad_in

    start = (jnp.zeros((D, FF), jnp.float32), jnp.zeros((D, FF), jnp.float32), jnp.zeros((FF, D), jnp.float32))
    sums, grad_tokens = lax.scan(one, start, jnp.arange(CAND, dtype=jnp.int32))
    return grad_tokens, sums[0], sums[1], sums[2]
```

```python
import functools

import jax
import jax.numpy as jnp
from jax import lax
from jax.experimental import pallas as pl
from jax.experimental.pallas import tpu as pltpu
from jax.sharding import PartitionSpec as P

F32, BF16 = jnp.float32, jnp.bfloat16
MESH = pl.DeviceIdType.MESH


def mm(a, b, ca, cb):
    return lax.dot_general(a, b, (((ca,), (cb,)), ((), ())), preferred_element_type=F32)


def kernel(
    nc, nh, keep_ref, tok_ref, cot_ref, gw_ref, uw_ref, dw_ref,
    gt_ref, gg_ref, gu_ref, gd_ref,
    xs, kbuf, psend, prcv, pown, ysend, yrcv, dbuf, accg, accu, accd, part, parr,
    lsem, s1s, s1r, xup, xdn, xcs, xr, ks, kr, ps, pr, ys, yr, ds, dr, qs, qr,
):
    c, h = lax.axis_index("cand"), lax.axis_index("hid")
    per = nh // nc
    rows = nh // per
    row, col = h // per, h % per
    groups = nc // 2
    grp, core = c // 2, c % 2
    sib = grp * 2 + 1 - core
    toks, dh = tok_ref.shape[1], tok_ref.shape[2]
    half = gw_ref.shape[1] // 2
    mine = pl.ds(pl.multiple_of(core * half, half), half)
    other = pl.ds(pl.multiple_of((1 - core) * half, half), half)

    def rcopy(src, dst, ssem, rsem, to):
        return pltpu.make_async_remote_copy(
            src_ref=src, dst_ref=dst, send_sem=ssem, recv_sem=rsem, device_id=to, device_id_type=MESH
        )

    barrier = pltpu.get_barrier_semaphore()

    @pl.loop(0, nh)
    def _(i):
        @pl.when(i != h)
        def _():
            pl.semaphore_signal(barrier, inc=1, device_id=(c, i), device_id_type=MESH)

        @pl.when((row != c) | (i != h))
        def _():
            pl.semaphore_signal(barrier, inc=1, device_id=(row, i), device_id_type=MESH)

    @pl.loop(0, nc)
    def _(i):
        @pl.when(i != c)
        def _():
            pl.semaphore_signal(barrier, inc=1, device_id=(i, h), device_id_type=MESH)

    own = jnp.where(row == c, 1, 0)
    pl.semaphore_wait(barrier, (nh - 1) + (nc - 1) + nh - own)

    def first(a, s):
        ref = (tok_ref, cot_ref)[a].at[0]
        return rcopy(ref, xs.at[s, col, a], s1s.at[a], s1r.at[s, a], (row, h))

    locals_ = [
        pltpu.make_async_copy(ref.at[0], xs.at[c, col, a], lsem.at[a])
        for a, ref in enumerate((tok_ref, cot_ref))
    ]

    @pl.when(row == c)
    def _():
        for cp in locals_:
            cp.start()

    @pl.when(row != c)
    def _():
        for a in range(2):
            first(a, c).start()

    def keep_copy(j):
        to = lax.rem(c + j, nc)
        return rcopy(keep_ref, kbuf.at[j], ks.at[j], kr.at[j], (to, h))

    for j in range(1, nc):
        keep_copy(j).start()
    kbuf[0] = keep_ref[...]

    accg[...] = jnp.zeros_like(accg)
    accu[...] = jnp.zeros_like(accu)
    accd[...] = jnp.zeros_like(accd)

    @pl.when(row == c)
    def _():
        for cp in locals_:
            cp.wait()

    def up_copy(s):
        return rcopy(xs.at[s, col], xs.at[s, col], xup.at[s], xr.at[s, col], (c, h + per))

    def down_copy(s):
        return rcopy(xs.at[s, col], xs.at[s, col], xdn.at[s], xr.at[s, col], (c, h - per))

    def col_copy(s, j):
        to = lax.rem(col + j, per)
        return rcopy(xs.at[s, col], xs.at[s, col], xcs.at[s, j], xr.at[s, col], (c, row * per + to))

    goes_up = (row >= c) & (row < rows - 1)
    goes_down = (row <= c) & (row > 0)

    def pass_on(s):
        @pl.when((row == c) & (s != c))
        def _():
            for a in range(2):
                first(a, s).wait_recv()

        @pl.when(row != c)
        def _():
            rcopy(xs.at[s, col], xs.at[s, col], xup.at[s], xr.at[s, col], (c, h)).wait_recv()

        @pl.when(goes_up)
        def _():
            up_copy(s).start()

        @pl.when(goes_down)
        def _():
            down_copy(s).start()

        for j in range(1, per):
            col_copy(s, j).start()

    def gathered(s, a):
        return jnp.concatenate([xs[s, i, a] for i in range(per)], axis=-1)

    def p_copy(s, a):
        return rcopy(psend.at[s, a], prcv.at[s, a], ps.at[s, a], pr.at[s, a], (sib, h))

    def y_copy(s, a, j):
        to = lax.rem(grp + j, groups) * 2 + core
        return rcopy(ysend.at[s, a], yrcv.at[j - 1, s, a], ys.at[j - 1, s, a], yr.at[j - 1, s, a], (to, h))

    def d_copy(s):
        return rcopy(dbuf.at[s, core], dbuf.at[s, core], ds.at[s], dr.at[s], (sib, h))

    def products(s, where):
        yield 0, mm(gathered(s, 0), gw_ref[:, where], 1, 0)
        yield 1, mm(gathered(s, 0), uw_ref[:, where], 1, 0)
        yield 2, mm(gathered(s, 1), dw_ref[where, :], 1, 1)

    @pl.loop(0, nc + 1)
    def _(t):
        @pl.when(t < nc)
        def _():
            pass_on(t)

        @pl.when(t >= 1)
        def _():
            s = t - 1
            for j in range(1, per):
                oc = lax.rem(col + j, per)
                rcopy(xs.at[s, oc], xs.at[s, oc], xcs.at[s, j], xr.at[s, oc], (c, h)).wait_recv()
            for a, p in products(s, other):
                psend[s, a] = p.astype(BF16)
                p_copy(s, a).start()
            for a, p in products(s, mine):
                pown[s, a] = p
            for a in range(3):
                p_copy(s, a).wait_recv()

                @pl.loop(0, toks // 64)
                def _(i):
                    at = pl.ds(pl.multiple_of(i * 64, 64), 64)
                    both = pown[s, a, at, :] + prcv[s, a, at, :].astype(F32)
                    pown[s, a, at, :] = both
                    ysend[s, a, at, :] = both.astype(BF16)

                for j in range(1, groups):
                    y_copy(s, a, j).start()

    for j in range(1, nc):
        keep_copy(j).wait()

    def part_copy(s, i):
        return rcopy(part.at[s, i], parr.at[h], qs.at[s, i], qr.at[h], (s, c * per + i))

    def stays(s, i):
        return (s == c) & (h == c * per + i)

    @pl.loop(0, nc)
    def _(s):
        for a in range(3):
            for j in range(1, groups):
                y_copy(s, a, j).wait_recv()
        keep = kbuf[lax.rem(c - s + nc, nc), 0:1, 0:1]

        @pl.loop(0, toks // 16)
        def _(i):
            at = pl.ds(pl.multiple_of(i * 16, 16), 16)
            total = [pown[s, a, at, :] for a in range(3)]
            for j in range(groups - 1):
                total = [total[a] + yrcv[j, s, a, at, :].astype(F32) for a in range(3)]
            gate, up, dhid = total
            sig = jax.nn.sigmoid(gate)
            act = keep * gate * sig
            dhid = keep * dhid
            dbuf[s, core, 0, at, :] = (act * up).astype(BF16)
            dbuf[s, core, 1, at, :] = (dhid * act).astype(BF16)
            dbuf[s, core, 2, at, :] = (dhid * up * keep * sig * (1.0 + gate * (1.0 - sig))).astype(BF16)

        d_copy(s).start()
        rcopy(dbuf.at[s, 1 - core], dbuf.at[s, 1 - core], ds.at[s], dr.at[s], (sib, h)).wait_recv()

        for i in range(per):
            at = slice(i * dh, (i + 1) * dh)
            piece = sum(
                mm(dbuf[s, k, a], w[at, k * half:(k + 1) * half], 1, 1)
                for k in range(2)
                for a, w in ((2, gw_ref), (1, uw_ref))
            )
            part[s, i] = piece.astype(BF16)

            @pl.when(stays(s, i))
            def _():
                cp = pltpu.make_async_copy(part.at[s, i], parr.at[h], lsem.at[0])
                cp.start()
                cp.wait()

            @pl.when(jnp.logical_not(stays(s, i)))
            def _():
                part_copy(s, i).start()

        for k in range(2):
            at = slice(k * half, (k + 1) * half)
            accg[:, at] += mm(gathered(s, 0), dbuf[s, k, 2], 0, 0)
            accu[:, at] += mm(gathered(s, 0), dbuf[s, k, 1], 0, 0)
            accd[at, :] += mm(dbuf[s, k, 0], gathered(s, 1), 0, 0)

    gg_ref[...] = accg[...].astype(BF16)
    gu_ref[...] = accu[...].astype(BF16)
    gd_ref[...] = accd[...].astype(BF16)

    for i in range(nh):
        @pl.when((row != c) | (h != i))
        def _():
            rcopy(parr.at[i], parr.at[i], qs.at[0, 0], qr.at[i], (c, h)).wait_recv()

    gt_ref[0] = sum(parr[i].astype(F32) for i in range(nh))

    @pl.when(row != c)
    def _():
        for a in range(2):
            first(a, c).wait_send()

    @pl.loop(0, nc)
    def _(s):
        @pl.when(goes_up)
        def _():
            up_copy(s).wait_send()

        @pl.when(goes_down)
        def _():
            down_copy(s).wait_send()

        for j in range(1, per):
            col_copy(s, j).wait_send()
        for a in range(3):
            p_copy(s, a).wait_send()
            for j in range(1, groups):
                y_copy(s, a, j).wait_send()
        d_copy(s).wait_send()
        for i in range(per):
            @pl.when(jnp.logical_not(stays(s, i)))
            def _():
                part_copy(s, i).wait_send()


def shards(nc, nh, tokens, cotangent, gate_weight, up_weight, down_weight, width_steps, block_order):
    width = gate_weight.shape[1]
    ff = width * nh
    places = jnp.arange(nh, dtype=jnp.int32)
    logical = jnp.sum(jnp.where(places == lax.axis_index("hid"), block_order, 0))
    active = logical * width < width_steps[0] * (ff // 8)
    keep = jnp.broadcast_to(active.astype(F32), (8, 128))
    toks, dh = tokens.shape[1:]
    dq, half = gate_weight.shape[0], width // 2
    per, groups = nh // nc, nc // 2
    sem = pltpu.SemaphoreType.DMA
    vm = pltpu.VMEM
    vspec = pl.BlockSpec(memory_space=pltpu.VMEM)
    out = jax.ShapeDtypeStruct
    gt, gg, gu, gd = pl.pallas_call(
        functools.partial(kernel, nc, nh),
        out_shape=(
            out((1, toks, dh), F32), out((dq, width), BF16), out((dq, width), BF16), out((width, dq), BF16),
        ),
        in_specs=[vspec] * 6,
        out_specs=(vspec,) * 4,
        scratch_shapes=[
            vm((nc, per, 2, toks, dh), BF16),
            vm((nc, 8, 128), F32),
            vm((nc, 3, toks, half), BF16),
            vm((nc, 3, toks, half), BF16),
            vm((nc, 3, toks, half), F32),
            vm((nc, 3, toks, half), BF16),
            vm((groups - 1, nc, 3, toks, half), BF16),
            vm((nc, 2, 3, toks, half), BF16),
            vm((dq, width), F32),
            vm((dq, width), F32),
            vm((width, dq), F32),
            vm((nc, per, toks, dh), BF16),
            vm((nh, toks, dh), BF16),
            sem((2,)), sem((2,)), sem((nc, 2)), sem((nc,)), sem((nc,)), sem((nc, per)), sem((nc, per)),
            sem((nc,)), sem((nc,)), sem((nc, 3)), sem((nc, 3)),
            sem((groups - 1, nc, 3)), sem((groups - 1, nc, 3)), sem((nc,)), sem((nc,)),
            sem((nc, per)), sem((nh,)),
        ],
        compiler_params=pltpu.CompilerParams(
            collective_id=0, has_side_effects=True, vmem_limit_bytes=67043328
        ),
    )(keep, tokens, cotangent, gate_weight, up_weight, down_weight)
    return gt, gg.astype(F32), gu.astype(F32), gd.astype(F32)


def solution(mesh):
    in_specs = (
        P("cand", None, "hid"),
        P("cand", None, "hid"),
        P("cand", "hid"),
        P("cand", "hid"),
        P("hid", "cand"),
        P("cand"),
        P(),
    )
    out_specs = (P("cand", None, "hid"), P("cand", "hid"), P("cand", "hid"), P("hid", "cand"))
    body = functools.partial(shards, mesh.shape["cand"], mesh.shape["hid"])
    return jax.shard_map(body, mesh=mesh, in_specs=in_specs, out_specs=out_specs, check_vma=False)
```

```python
import functools

import jax
import jax.numpy as jnp
from jax import lax
from jax.experimental import pallas as pl
from jax.experimental.pallas import tpu as pltpu
from jax.sharding import PartitionSpec as P

F32, BF16 = jnp.float32, jnp.bfloat16
MESH = pl.DeviceIdType.MESH


def mm(a, b, ca, cb):
    return lax.dot_general(a, b, (((ca,), (cb,)), ((), ())), preferred_element_type=F32)


def kernel(
    nc, nh, ns, slots, ws_ref, bo_ref, tok_ref, cot_ref, gw_hbm, uw_hbm, dw_hbm,
    gt_ref, gg_ref, gu_ref, gd_ref,
    gw_ref, uw_ref, dw_ref, kown, xs, kbuf, psend, prcv, pown, ysend, yrcv, dbuf, accg, accu, accd,
    part, rbuf, red, fin,
    wsem, lsem, s1s, s1r, xup, xdn, xcs, xr, ks, kr, ps, pr, ys, yr, ds, dr, qs, qr, fs, fr, cred,
):
    c, h = lax.axis_index("cand"), lax.axis_index("hid")
    per = nh // nc
    rows = nh // per
    row, col = h // per, h % per
    groups = nc // 2
    grp, core = c // 2, c % 2
    sib = grp * 2 + 1 - core
    toks, dh = tok_ref.shape[1], tok_ref.shape[2]
    tk = toks // ns
    nk = nc * ns
    width = gw_ref.shape[1]
    half = width // 2
    mine = pl.ds(pl.multiple_of(core * half, half), half)
    other = pl.ds(pl.multiple_of((1 - core) * half, half), half)

    def rcopy(src, dst, ssem, rsem, to):
        return pltpu.make_async_remote_copy(
            src_ref=src, dst_ref=dst, send_sem=ssem, recv_sem=rsem, device_id=to, device_id_type=MESH
        )

    loads = [
        pltpu.make_async_copy(src, dst, wsem.at[a])
        for a, (src, dst) in enumerate(((gw_hbm, gw_ref), (uw_hbm, uw_ref), (dw_hbm, dw_ref)))
    ]

    barrier = pltpu.get_barrier_semaphore()

    @pl.loop(0, nh)
    def _(i):
        @pl.when(i != h)
        def _():
            pl.semaphore_signal(barrier, inc=1, device_id=(c, i), device_id_type=MESH)

    @pl.loop(0, nc)
    def _(i):
        @pl.when(i != c)
        def _():
            pl.semaphore_signal(barrier, inc=1, device_id=(i, h), device_id_type=MESH)

    def local(t):
        a, f = t // ns, t % ns
        ref = (tok_ref, cot_ref)[a].at[0, f * tk:(f + 1) * tk]
        return pltpu.make_async_copy(ref, xs.at[c * ns + f, col, a], lsem.at[t])

    @pl.when(row == c)
    def _():
        for t in range(2 * ns):
            local(t).start()

    for cp in loads:
        cp.start()
    level = bo_ref[h] * width - ws_ref[0] * (width * nh // 8)
    kown[...] = jnp.where(jnp.full(kown.shape, level, jnp.int32) < 0, 1.0, 0.0).astype(F32)
    kbuf[0] = kown[...]

    pl.semaphore_wait(barrier, (nh - 1) + (nc - 1))

    def first(a, f, s):
        ref = (tok_ref, cot_ref)[a].at[0, f * tk:(f + 1) * tk]
        k = s * ns + f
        return rcopy(ref, xs.at[k, col, a], s1s.at[f, a], s1r.at[k, a], (row, h))

    @pl.when(row != c)
    def _():
        for f in range(ns):
            for a in range(2):
                first(a, f, c).start()

    def keep_copy(j):
        to = lax.rem(c + j, nc)
        return rcopy(kown, kbuf.at[j], ks.at[j], kr.at[j], (to, h))

    accg[...] = jnp.zeros_like(accg)
    accu[...] = jnp.zeros_like(accu)
    accd[...] = jnp.zeros_like(accd)

    @pl.when(row == c)
    def _():
        for t in range(2 * ns):
            local(t).wait()

    for cp in loads:
        cp.wait()

    def up_copy(k):
        return rcopy(xs.at[k, col], xs.at[k, col], xup.at[k], xr.at[k, col], (c, h + per))

    def down_copy(k):
        return rcopy(xs.at[k, col], xs.at[k, col], xdn.at[k], xr.at[k, col], (c, h - per))

    def col_copy(k, j):
        to = lax.rem(col + j, per)
        return rcopy(xs.at[k, col], xs.at[k, col], xcs.at[k, j], xr.at[k, col], (c, row * per + to))

    goes_up = (row >= c) & (row < rows - 1)
    goes_down = (row <= c) & (row > 0)

    def pass_on(k):
        s = k // ns

        @pl.when((row == c) & (s != c))
        def _():
            for a in range(2):
                rcopy(xs.at[k, col, a], xs.at[k, col, a], s1s.at[0, a], s1r.at[k, a], (c, h)).wait_recv()

        @pl.when(row != c)
        def _():
            rcopy(xs.at[k, col], xs.at[k, col], xup.at[k], xr.at[k, col], (c, h)).wait_recv()

        @pl.when(goes_up)
        def _():
            up_copy(k).start()

        @pl.when(goes_down)
        def _():
            down_copy(k).start()

        for j in range(1, per):
            col_copy(k, j).start()

    def gathered(k, a):
        return jnp.concatenate([xs[k, i, a] for i in range(per)], axis=-1)

    def gathered_all(s, a):
        return jnp.concatenate([gathered(s * ns + f, a) for f in range(ns)], axis=0)

    def p_copy(k, a):
        return rcopy(psend.at[k, a], prcv.at[k, a], ps.at[k, a], pr.at[k, a], (sib, h))

    def y_copy(k, a, j):
        to = lax.rem(grp + j, groups) * 2 + core
        return rcopy(ysend.at[k, a], yrcv.at[j - 1, k, a], ys.at[j - 1, k, a], yr.at[j - 1, k, a], (to, h))

    def products(k, where):
        yield 0, mm(gathered(k, 0), gw_ref[:, where], 1, 0)
        yield 1, mm(gathered(k, 0), uw_ref[:, where], 1, 0)
        yield 2, mm(gathered(k, 1), dw_ref[where, :], 1, 1)

    def chunk(t, lead):
        return lax.rem(lead * 2 * ns + t, nk)

    @pl.loop(0, nk + 1)
    def _(t):
        @pl.when(t < nk)
        def _():
            pass_on(chunk(t, grp))

        @pl.when(t >= 1)
        def _():
            k = chunk(t - 1, grp)
            for j in range(1, per):
                oc = lax.rem(col + j, per)
                rcopy(xs.at[k, oc], xs.at[k, oc], xcs.at[k, j], xr.at[k, oc], (c, h)).wait_recv()
            for a, p in products(k, other):
                psend[k, a] = p.astype(BF16)
                p_copy(k, a).start()
            for a, p in products(k, mine):
                pown[k, a] = p
            for a in range(3):
                p_copy(k, a).wait_recv()

                @pl.loop(0, tk // 32)
                def _(i):
                    at = pl.ds(pl.multiple_of(i * 32, 32), 32)
                    both = pown[k, a, at, :] + prcv[k, a, at, :].astype(F32)
                    pown[k, a, at, :] = both
                    ysend[k, a, at, :] = both.astype(BF16)

                for j in range(1, groups):
                    y_copy(k, a, j).start()

    for j in range(1, nc):
        keep_copy(j).start()
    for j in range(1, nc):
        keep_copy(j).wait()

    def d_rows(k):
        return k // ns, pl.ds(pl.multiple_of(lax.rem(k, ns) * tk, tk), tk)

    def d_copy(k, who):
        s, at = d_rows(k)
        ref = dbuf.at[s, who, :, at]
        return rcopy(ref, ref, ds.at[k], dr.at[k], (sib, h))

    def part_copy(t, k, i):
        at = lax.rem(t, slots)
        return rcopy(part.at[k, i], rbuf.at[at, h], qs.at[k, i], qr.at[at, h], (c, c * per + i))

    def stays(i):
        return h == c * per + i

    def fin_copy(k):
        f = lax.rem(k, ns)
        return rcopy(red.at[k], fin.at[f], fs.at[k], fr.at[f], (k // ns, h))

    def collect(t):
        k, at = chunk(t, nxt), lax.rem(t, slots)

        @pl.when(row == c)
        def _():
            @pl.loop(0, nh)
            def _(i):
                @pl.when(i != h)
                def _():
                    rcopy(rbuf.at[at, i], rbuf.at[at, i], qs.at[k, 0], qr.at[at, i], (c, h)).wait_recv()

            red[k] = sum(rbuf[at, i].astype(F32) for i in range(nh)).astype(BF16)

            if slots < nk:
                @pl.loop(0, nh)
                def _(i):
                    @pl.when((i != h) & (t < nk - slots))
                    def _():
                        pl.semaphore_signal(cred.at[col], inc=1, device_id=(c, i), device_id_type=MESH)

            @pl.when(k // ns == c)
            def _():
                fin[lax.rem(k, ns)] = red[k]

            @pl.when(k // ns != c)
            def _():
                fin_copy(k).start()

    lag = 2
    nxt = lax.rem(grp + 1, groups)

    @pl.loop(0, nk)
    def _(t):
        k = chunk(t, nxt)
        s, half_rows = d_rows(k)
        for a in range(3):
            for j in range(1, groups):
                y_copy(k, a, j).wait_recv()
        keep = kbuf[lax.rem(c - s + nc, nc), 0:1, 0:1]

        @pl.loop(0, tk // 16)
        def _(i):
            at = pl.ds(pl.multiple_of(i * 16, 16), 16)
            to = pl.ds(pl.multiple_of(lax.rem(k, ns) * tk + i * 16, 16), 16)
            total = [pown[k, a, at, :] for a in range(3)]
            for j in range(groups - 1):
                total = [total[a] + yrcv[j, k, a, at, :].astype(F32) for a in range(3)]
            gate, up, dhid = total
            sig = jax.nn.sigmoid(gate)
            act = keep * gate * sig
            dhid = keep * dhid
            dbuf[s, core, 0, to, :] = (act * up).astype(BF16)
            dbuf[s, core, 1, to, :] = (dhid * act).astype(BF16)
            dbuf[s, core, 2, to, :] = (dhid * up * keep * sig * (1.0 + gate * (1.0 - sig))).astype(BF16)

        d_copy(k, core).start()
        d_copy(k, 1 - core).wait_recv()

        for i in range(per):
            at = slice(i * dh, (i + 1) * dh)
            piece = sum(
                mm(dbuf[s, b, a, half_rows, :], w[at, b * half:(b + 1) * half], 1, 1)
                for b in range(2)
                for a, w in ((2, gw_ref), (1, uw_ref))
            ).astype(BF16)

            @pl.when(stays(i))
            def _():
                rbuf[lax.rem(t, slots), h] = piece

            @pl.when(jnp.logical_not(stays(i)))
            def _():
                part[k, i] = piece
                if slots < nk:
                    @pl.when(t >= slots)
                    def _():
                        pl.semaphore_wait(cred.at[i], 1)

                part_copy(t, k, i).start()

        @pl.when(t >= lag)
        def _():
            collect(t - lag)

        @pl.when(lax.rem(t, ns) == ns - 1)
        def _():
            for b in range(2):
                at = slice(b * half, (b + 1) * half)
                accg[:, at] += mm(gathered_all(s, 0), dbuf[s, b, 2], 0, 0)
                accu[:, at] += mm(gathered_all(s, 0), dbuf[s, b, 1], 0, 0)
                accd[at, :] += mm(dbuf[s, b, 0], gathered_all(s, 1), 0, 0)

    for t in range(nk - lag, nk):
        collect(jnp.int32(t))

    gg_ref[...] = accg[...].astype(BF16)
    gu_ref[...] = accu[...].astype(BF16)
    gd_ref[...] = accd[...].astype(BF16)

    for f in range(ns):
        @pl.when(row != c)
        def _():
            rcopy(fin.at[f], fin.at[f], fs.at[0], fr.at[f], (c, h)).wait_recv()

        gt_ref[0, f * tk:(f + 1) * tk] = fin[f].astype(F32)

    @pl.when(row != c)
    def _():
        for f in range(ns):
            for a in range(2):
                first(a, f, c).wait_send()

    @pl.loop(0, nk)
    def _(k):
        @pl.when(goes_up)
        def _():
            up_copy(k).wait_send()

        @pl.when(goes_down)
        def _():
            down_copy(k).wait_send()

        for j in range(1, per):
            col_copy(k, j).wait_send()
        for a in range(3):
            p_copy(k, a).wait_send()
            for j in range(1, groups):
                y_copy(k, a, j).wait_send()
        d_copy(k, core).wait_send()
        for i in range(per):
            @pl.when(jnp.logical_not(stays(i)))
            def _():
                part_copy(k, k, i).wait_send()

        @pl.when((row == c) & (k // ns != c))
        def _():
            fin_copy(k).wait_send()


def shards(nc, nh, tokens, cotangent, gate_weight, up_weight, down_weight, width_steps, block_order):
    width = gate_weight.shape[1]
    toks, dh = tokens.shape[1:]
    dq, half = gate_weight.shape[0], width // 2
    per, groups = nh // nc, nc // 2
    ns = 2
    nk, tk = nc * ns, toks // ns
    slots = min(nk, (8 << 20) // (nh * tk * max(dh, 128) * 2))
    sem = pltpu.SemaphoreType.DMA
    vm = pltpu.VMEM
    vspec = pl.BlockSpec(memory_space=pltpu.VMEM)
    sspec = pl.BlockSpec(memory_space=pltpu.SMEM)
    anyspec = pl.BlockSpec(memory_space=pl.ANY)
    out = jax.ShapeDtypeStruct
    gt, gg, gu, gd = pl.pallas_call(
        functools.partial(kernel, nc, nh, ns, slots),
        out_shape=(
            out((1, toks, dh), F32), out((dq, width), BF16), out((dq, width), BF16), out((width, dq), BF16),
        ),
        in_specs=[sspec] * 2 + [anyspec] * 5,
        out_specs=(vspec,) * 4,
        scratch_shapes=[
            vm((dq, width), BF16),
            vm((dq, width), BF16),
            vm((width, dq), BF16),
            vm((8, 128), F32),
            vm((nk, per, 2, tk, dh), BF16),
            vm((nc, 8, 128), F32),
            vm((nk, 3, tk, half), BF16),
            vm((nk, 3, tk, half), BF16),
            vm((nk, 3, tk, half), F32),
            vm((nk, 3, tk, half), BF16),
            vm((groups - 1, nk, 3, tk, half), BF16),
            vm((nc, 2, 3, toks, half), BF16),
            vm((dq, width), F32),
            vm((dq, width), F32),
            vm((width, dq), F32),
            vm((nk, per, tk, dh), BF16),
            vm((slots, nh, tk, dh), BF16),
            vm((nk, tk, dh), BF16),
            vm((ns, tk, dh), BF16),
            sem((3,)), sem((2 * ns,)), sem((ns, 2)), sem((nk, 2)), sem((nk,)), sem((nk,)), sem((nk, per)),
            sem((nk, per)), sem((nc,)), sem((nc,)), sem((nk, 3)), sem((nk, 3)),
            sem((groups - 1, nk, 3)), sem((groups - 1, nk, 3)), sem((nk,)), sem((nk,)),
            sem((nk, per)), sem((slots, nh)), sem((nk,)), sem((ns,)), pltpu.SemaphoreType.REGULAR((per,)),
        ],
        compiler_params=pltpu.CompilerParams(
            collective_id=0, has_side_effects=True, vmem_limit_bytes=67043328
        ),
    )(width_steps, block_order, tokens, cotangent, gate_weight, up_weight, down_weight)
    return gt, gg.astype(F32), gu.astype(F32), gd.astype(F32)


def solution(mesh):
    in_specs = (
        P("cand", None, "hid"),
        P("cand", None, "hid"),
        P("cand", "hid"),
        P("cand", "hid"),
        P("hid", "cand"),
        P("cand"),
        P(),
    )
    out_specs = (P("cand", None, "hid"), P("cand", "hid"), P("cand", "hid"), P("hid", "cand"))
    body = functools.partial(shards, mesh.shape["cand"], mesh.shape["hid"])
    return jax.shard_map(body, mesh=mesh, in_specs=in_specs, out_specs=out_specs, check_vma=False)
```

```python
import functools

import jax
import jax.numpy as jnp
from jax import lax
from jax.experimental import pallas as pl
from jax.experimental.pallas import tpu as pltpu
from jax.sharding import PartitionSpec as P

F32, BF16 = jnp.float32, jnp.bfloat16
MESH = pl.DeviceIdType.MESH


def mm(a, b, ca, cb):
    return lax.dot_general(a, b, (((ca,), (cb,)), ((), ())), preferred_element_type=F32)


def kernel(
    nc, nh, ws_ref, bo_ref, tok_ref, cot_ref, gw_hbm, uw_hbm, dw_hbm,
    gt_ref, gg_ref, gu_ref, gd_ref,
    gw_ref, uw_ref, dw_ref, keep_ref, wsem, xs, kbuf, psend, prcv, pown, ysend, yrcv, dbuf, accg, accu, accd, part, parr,
    lsem, s1s, s1r, xup, xdn, xcs, xr, ks, kr, ps, pr, ys, yr, ds, dr, qs, qr,
):
    c, h = lax.axis_index("cand"), lax.axis_index("hid")
    per = nh // nc
    rows = nh // per
    row, col = h // per, h % per
    groups = nc // 2
    grp, core = c // 2, c % 2
    sib = grp * 2 + 1 - core
    toks, dh = tok_ref.shape[1], tok_ref.shape[2]
    half = gw_ref.shape[1] // 2
    mine = pl.ds(pl.multiple_of(core * half, half), half)
    other = pl.ds(pl.multiple_of((1 - core) * half, half), half)

    def rcopy(src, dst, ssem, rsem, to):
        return pltpu.make_async_remote_copy(
            src_ref=src, dst_ref=dst, send_sem=ssem, recv_sem=rsem, device_id=to, device_id_type=MESH
        )

    loads = [
        pltpu.make_async_copy(src, dst, wsem.at[a])
        for a, (src, dst) in enumerate(((gw_hbm, gw_ref), (uw_hbm, uw_ref), (dw_hbm, dw_ref)))
    ]
    for cp in loads:
        cp.start()
    width = gw_ref.shape[1]
    level = bo_ref[h] * width - ws_ref[0] * (width * nh // 8)
    keep_ref[...] = jnp.where(jnp.full(keep_ref.shape, level, jnp.int32) < 0, 1.0, 0.0).astype(F32)

    barrier = pltpu.get_barrier_semaphore()

    @pl.loop(0, nh)
    def _(i):
        @pl.when(i != h)
        def _():
            pl.semaphore_signal(barrier, inc=1, device_id=(c, i), device_id_type=MESH)

        @pl.when((row != c) | (i != h))
        def _():
            pl.semaphore_signal(barrier, inc=1, device_id=(row, i), device_id_type=MESH)

    @pl.loop(0, nc)
    def _(i):
        @pl.when(i != c)
        def _():
            pl.semaphore_signal(barrier, inc=1, device_id=(i, h), device_id_type=MESH)

    own = jnp.where(row == c, 1, 0)
    pl.semaphore_wait(barrier, (nh - 1) + (nc - 1) + nh - own)

    def first(a, s):
        ref = (tok_ref, cot_ref)[a].at[0]
        return rcopy(ref, xs.at[s, col, a], s1s.at[a], s1r.at[s, a], (row, h))

    locals_ = [
        pltpu.make_async_copy(ref.at[0], xs.at[c, col, a], lsem.at[a])
        for a, ref in enumerate((tok_ref, cot_ref))
    ]

    @pl.when(row == c)
    def _():
        for cp in locals_:
            cp.start()

    @pl.when(row != c)
    def _():
        for a in range(2):
            first(a, c).start()

    def keep_copy(j):
        to = lax.rem(c + j, nc)
        return rcopy(keep_ref, kbuf.at[j], ks.at[j], kr.at[j], (to, h))

    for j in range(1, nc):
        keep_copy(j).start()
    kbuf[0] = keep_ref[...]

    accg[...] = jnp.zeros_like(accg)
    accu[...] = jnp.zeros_like(accu)
    accd[...] = jnp.zeros_like(accd)
    for cp in loads:
        cp.wait()

    @pl.when(row == c)
    def _():
        for cp in locals_:
            cp.wait()

    def up_copy(s):
        return rcopy(xs.at[s, col], xs.at[s, col], xup.at[s], xr.at[s, col], (c, h + per))

    def down_copy(s):
        return rcopy(xs.at[s, col], xs.at[s, col], xdn.at[s], xr.at[s, col], (c, h - per))

    def col_copy(s, j):
        to = lax.rem(col + j, per)
        return rcopy(xs.at[s, col], xs.at[s, col], xcs.at[s, j], xr.at[s, col], (c, row * per + to))

    goes_up = (row >= c) & (row < rows - 1)
    goes_down = (row <= c) & (row > 0)

    def pass_on(s):
        @pl.when((row == c) & (s != c))
        def _():
            for a in range(2):
                first(a, s).wait_recv()

        @pl.when(row != c)
        def _():
            rcopy(xs.at[s, col], xs.at[s, col], xup.at[s], xr.at[s, col], (c, h)).wait_recv()

        @pl.when(goes_up)
        def _():
            up_copy(s).start()

        @pl.when(goes_down)
        def _():
            down_copy(s).start()

        for j in range(1, per):
            col_copy(s, j).start()

    def gathered(s, a):
        return jnp.concatenate([xs[s, i, a] for i in range(per)], axis=-1)

    def p_copy(s, a):
        return rcopy(psend.at[s, a], prcv.at[s, a], ps.at[s, a], pr.at[s, a], (sib, h))

    def y_copy(s, a, j):
        to = lax.rem(grp + j, groups) * 2 + core
        return rcopy(ysend.at[s, a], yrcv.at[j - 1, s, a], ys.at[j - 1, s, a], yr.at[j - 1, s, a], (to, h))

    def d_copy(s):
        return rcopy(dbuf.at[s, core], dbuf.at[s, core], ds.at[s], dr.at[s], (sib, h))

    def products(s, where):
        yield 0, mm(gathered(s, 0), gw_ref[:, where], 1, 0)
        yield 1, mm(gathered(s, 0), uw_ref[:, where], 1, 0)
        yield 2, mm(gathered(s, 1), dw_ref[where, :], 1, 1)

    @pl.loop(0, nc + 1)
    def _(t):
        @pl.when(t < nc)
        def _():
            pass_on(lax.rem(grp * 2 + t, nc))

        @pl.when(t >= 1)
        def _():
            s = lax.rem(grp * 2 + t - 1, nc)
            for j in range(1, per):
                oc = lax.rem(col + j, per)
                rcopy(xs.at[s, oc], xs.at[s, oc], xcs.at[s, j], xr.at[s, oc], (c, h)).wait_recv()
            for a, p in products(s, other):
                psend[s, a] = p.astype(BF16)
                p_copy(s, a).start()
            for a, p in products(s, mine):
                pown[s, a] = p
            for a in range(3):
                p_copy(s, a).wait_recv()

                @pl.loop(0, toks // 64)
                def _(i):
                    at = pl.ds(pl.multiple_of(i * 64, 64), 64)
                    both = pown[s, a, at, :] + prcv[s, a, at, :].astype(F32)
                    pown[s, a, at, :] = both
                    ysend[s, a, at, :] = both.astype(BF16)

                for j in range(1, groups):
                    y_copy(s, a, j).start()

    for j in range(1, nc):
        keep_copy(j).wait()

    def part_copy(s, i):
        return rcopy(part.at[s, i], parr.at[h], qs.at[s, i], qr.at[h], (s, c * per + i))

    def stays(s, i):
        return (s == c) & (h == c * per + i)

    nxt = lax.rem(grp + 1, groups)

    @pl.loop(0, nc)
    def _(t):
        s = lax.rem(nxt * 2 + t, nc)
        for a in range(3):
            for j in range(1, groups):
                y_copy(s, a, j).wait_recv()
        keep = kbuf[lax.rem(c - s + nc, nc), 0:1, 0:1]

        @pl.loop(0, toks // 16)
        def _(i):
            at = pl.ds(pl.multiple_of(i * 16, 16), 16)
            total = [pown[s, a, at, :] for a in range(3)]
            for j in range(groups - 1):
                total = [total[a] + yrcv[j, s, a, at, :].astype(F32) for a in range(3)]
            gate, up, dhid = total
            sig = jax.nn.sigmoid(gate)
            act = keep * gate * sig
            dhid = keep * dhid
            dbuf[s, core, 0, at, :] = (act * up).astype(BF16)
            dbuf[s, core, 1, at, :] = (dhid * act).astype(BF16)
            dbuf[s, core, 2, at, :] = (dhid * up * keep * sig * (1.0 + gate * (1.0 - sig))).astype(BF16)

        d_copy(s).start()
        rcopy(dbuf.at[s, 1 - core], dbuf.at[s, 1 - core], ds.at[s], dr.at[s], (sib, h)).wait_recv()

        for i in range(per):
            at = slice(i * dh, (i + 1) * dh)
            piece = sum(
                mm(dbuf[s, k, a], w[at, k * half:(k + 1) * half], 1, 1)
                for k in range(2)
                for a, w in ((2, gw_ref), (1, uw_ref))
            )
            part[s, i] = piece.astype(BF16)

            @pl.when(stays(s, i))
            def _():
                cp = pltpu.make_async_copy(part.at[s, i], parr.at[h], lsem.at[0])
                cp.start()
                cp.wait()

            @pl.when(jnp.logical_not(stays(s, i)))
            def _():
                part_copy(s, i).start()

        for k in range(2):
            at = slice(k * half, (k + 1) * half)
            accg[:, at] += mm(gathered(s, 0), dbuf[s, k, 2], 0, 0)
            accu[:, at] += mm(gathered(s, 0), dbuf[s, k, 1], 0, 0)
            accd[at, :] += mm(dbuf[s, k, 0], gathered(s, 1), 0, 0)

    gg_ref[...] = accg[...].astype(BF16)
    gu_ref[...] = accu[...].astype(BF16)
    gd_ref[...] = accd[...].astype(BF16)

    for i in range(nh):
        @pl.when((row != c) | (h != i))
        def _():
            rcopy(parr.at[i], parr.at[i], qs.at[0, 0], qr.at[i], (c, h)).wait_recv()

    gt_ref[0] = sum(parr[i].astype(F32) for i in range(nh))

    @pl.when(row != c)
    def _():
        for a in range(2):
            first(a, c).wait_send()

    @pl.loop(0, nc)
    def _(s):
        @pl.when(goes_up)
        def _():
            up_copy(s).wait_send()

        @pl.when(goes_down)
        def _():
            down_copy(s).wait_send()

        for j in range(1, per):
            col_copy(s, j).wait_send()
        for a in range(3):
            p_copy(s, a).wait_send()
            for j in range(1, groups):
                y_copy(s, a, j).wait_send()
        d_copy(s).wait_send()
        for i in range(per):
            @pl.when(jnp.logical_not(stays(s, i)))
            def _():
                part_copy(s, i).wait_send()


def shards(nc, nh, tokens, cotangent, gate_weight, up_weight, down_weight, width_steps, block_order):
    width = gate_weight.shape[1]
    toks, dh = tokens.shape[1:]
    dq, half = gate_weight.shape[0], width // 2
    per, groups = nh // nc, nc // 2
    sem = pltpu.SemaphoreType.DMA
    vm = pltpu.VMEM
    vspec = pl.BlockSpec(memory_space=pltpu.VMEM)
    out = jax.ShapeDtypeStruct
    gt, gg, gu, gd = pl.pallas_call(
        functools.partial(kernel, nc, nh),
        out_shape=(
            out((1, toks, dh), F32), out((dq, width), BF16), out((dq, width), BF16), out((width, dq), BF16),
        ),
        in_specs=[pl.BlockSpec(memory_space=pltpu.SMEM)] * 2 + [pl.BlockSpec(memory_space=pl.ANY)] * 5,
        out_specs=(vspec,) * 4,
        scratch_shapes=[
            vm((dq, width), BF16), vm((dq, width), BF16), vm((width, dq), BF16), vm((8, 128), F32), sem((3,)),
            vm((nc, per, 2, toks, dh), BF16),
            vm((nc, 8, 128), F32),
            vm((nc, 3, toks, half), BF16),
            vm((nc, 3, toks, half), BF16),
            vm((nc, 3, toks, half), F32),
            vm((nc, 3, toks, half), BF16),
            vm((groups - 1, nc, 3, toks, half), BF16),
            vm((nc, 2, 3, toks, half), BF16),
            vm((dq, width), F32),
            vm((dq, width), F32),
            vm((width, dq), F32),
            vm((nc, per, toks, dh), BF16),
            vm((nh, toks, dh), BF16),
            sem((2,)), sem((2,)), sem((nc, 2)), sem((nc,)), sem((nc,)), sem((nc, per)), sem((nc, per)),
            sem((nc,)), sem((nc,)), sem((nc, 3)), sem((nc, 3)),
            sem((groups - 1, nc, 3)), sem((groups - 1, nc, 3)), sem((nc,)), sem((nc,)),
            sem((nc, per)), sem((nh,)),
        ],
        compiler_params=pltpu.CompilerParams(
            collective_id=0, has_side_effects=True, vmem_limit_bytes=67043328
        ),
    )(width_steps, block_order, tokens, cotangent, gate_weight, up_weight, down_weight)
    return gt, gg.astype(F32), gu.astype(F32), gd.astype(F32)


def solution(mesh):
    in_specs = (
        P("cand", None, "hid"),
        P("cand", None, "hid"),
        P("cand", "hid"),
        P("cand", "hid"),
        P("hid", "cand"),
        P("cand"),
        P(),
    )
    out_specs = (P("cand", None, "hid"), P("cand", "hid"), P("cand", "hid"), P("hid", "cand"))
    body = functools.partial(shards, mesh.shape["cand"], mesh.shape["hid"])
    return jax.shard_map(body, mesh=mesh, in_specs=in_specs, out_specs=out_specs, check_vma=False)
```
